32 devices in a mesh: row: 4 (over y, core), col: 8 (over z, x).
Axes of the slice: x: 2, y: 2, z: 4, core: 2. Of those that a mesh axis runs over, the one named last changes fastest.
Arguments:
- front: float32 [12288, 12288], P('row', 'col'), may hold values from -6 to 6
- delayed: float32 [64, 12288], P('col', 'row'), may hold values from -6 to 6
- dest: int32 [64], P('col'), may hold values from 0 to 1023, as said below
- pivots: int32 [1024], replicated, may hold values from 0 to 12287, as said below
- pair_flags: int32 [1024], replicated, may hold values from 0 to 1, as said below
- linv: float32 [4, 256, 256], replicated, as said below
- dinv_diag: float32 [1024], replicated, may hold values from -0.1 to 0.1
- dinv_off: float32 [1024], replicated, may hold values from -0.08 to 0.08
Outputs:
- trailing: float32 [12288, 12288], P('row', 'col')
- factor: float32 [12288, 1024], P('row')
The draws below stay inside these ranges and needn't reach their ends.
Inputs may be any that keep to these rules, and one draw needn't show every extreme that they name: Distinct front columns; slots p * 256 to (p + 1) * 256 - 1 are panel p's pivots. Each block of 1536 columns held by one index of col contains exactly 128 of them. `pair_flags`: A 1 at slot s joins slots s and s + 1 into one 2x2 block; no two 1s are adjacent and the last slot of a panel holds 0. `dest`: several delayed columns may share a slot. Of the 8 delayed columns held by one index of col, at most 2 go to pivot columns held by the same index of col. `linv`: each panel's matrix is unit lower triangular: ones on the diagonal, zeros above it.
All inputs are finite; a program needn't handle non-finite values.
Results may differ from the reference program's by a relative error of at most 0.00015.
Values sent between devices are 32-bit elements; how exact they have to be, the bound alone decides.
A program may use at most 192 MiB of HBM per device.

```python
import jax
import jax.numpy as jnp
from jax import lax

NF = 12288
PANEL = 256
PANELS = 4
DEL_COL = 8
CAP = 2
CB = 1536
E = 1024
PIV_OWN = 128
NDEL = 64
N_COL = 8


def pivot_layout(key):
    base = jax.random.fold_in(key, 7)
    picks = jax.vmap(lambda owner: jax.random.permutation(jax.random.fold_in(base, owner), CB)[:PIV_OWN].astype(jnp.int32) + owner * CB)(jnp.arange(N_COL, dtype=jnp.int32))
    listed = picks.reshape(-1).astype(jnp.int32)
    order = jax.random.permutation(jax.random.fold_in(key, 11), E).astype(jnp.int32)
    placed = jnp.zeros((E,), jnp.int32).at[order].set(listed)
    return (placed, order.reshape(N_COL, PIV_OWN))


def draw_pivots(key, part):
    return pivot_layout(key)[0]


def draw_dest(key, part):
    placed, slot_table = pivot_layout(key)
    inner = jax.random.fold_in(key, 23)
    heavy = jax.random.randint(jax.random.fold_in(inner, 1), (), 0, N_COL).astype(jnp.int32)
    shifts = jax.random.randint(jax.random.fold_in(inner, 2), (N_COL,), 0, N_COL - 1).astype(jnp.int32)
    position = jnp.arange(DEL_COL, dtype=jnp.int32)
    others = (heavy + 1 + (shifts[:, None] + position[None, :] - CAP) % (N_COL - 1)) % N_COL
    owners = jnp.where(position[None, :] < CAP, heavy, others)
    choose = jax.random.randint(jax.random.fold_in(inner, 3), (N_COL, DEL_COL), 0, PIV_OWN).astype(jnp.int32)
    return slot_table[owners, choose].reshape(-1).astype(jnp.int32)


def draw_pair_flags(key, part):
    wanted = jax.random.randint(key, (E,), 0, 5) < 2
    closing = jnp.arange(E) % PANEL == PANEL - 1

    def advance(previous, inputs):
        want_here, close_here = inputs
        result = jnp.where(want_here & (previous == 0) & jnp.logical_not(close_here), 1, 0).astype(jnp.int32)
        return (result, result)
    _, flags_out = lax.scan(advance, jnp.int32(0), (wanted, closing))
    return flags_out


def draw_linv(key, part):
    values = 0.05 * jax.random.normal(key, (PANELS, PANEL, PANEL), jnp.float32)
    lower = jnp.arange(PANEL)[:, None] > jnp.arange(PANEL)[None, :]
    return jnp.where(lower[None], values, 0.0) + jnp.eye(PANEL, dtype=jnp.float32)[None]


def steps_of(rng, shape, pieces, smallest, top_value):
    def one(dim, shards_of):
        steps = jax.random.uniform(jax.random.fold_in(jax.random.fold_in(rng, 6), dim), (shards_of,), jnp.float32, smallest / len(pieces), top_value / len(pieces))
        return jnp.repeat(jnp.exp(steps), shape[dim] // shards_of).reshape((-1,) + (1,) * (len(shape) - dim - 1))

    level = one(*pieces[0])
    for cut in pieces[1:]:
        level = level * one(*cut)
    return level


def noise(key, shape, deviation, reach, cuts=(), held_as=jnp.bfloat16):
    gain = steps_of(key, shape, cuts, -0.22, 0.18) if cuts else 1.0
    values = jax.random.normal(key, shape, jnp.float32) * deviation * gain
    return jnp.minimum(jnp.maximum(values, -reach), reach).astype(held_as)


def setup_inputs(seed: int = 0) -> dict:
    streams_of = jax.random.split(jax.random.key(seed), 9)
    front = noise(streams_of[0], (NF, NF), 1.0, 6.0, ((0, 4), (1, 8)), jnp.float32)
    delayed = noise(streams_of[1], (NDEL, NF), 1.0, 6.0, ((0, 8), (1, 4)), jnp.float32)
    dest = draw_dest(jax.random.fold_in(streams_of[8], 71), 0)
    pivots = draw_pivots(jax.random.fold_in(streams_of[8], 71), 0)
    pair_flags = draw_pair_flags(jax.random.fold_in(streams_of[8], 71), 0)
    linv = draw_linv(jax.random.fold_in(streams_of[8], 71), 0)
    dinv_diag = jnp.clip(jax.random.uniform(streams_of[6], (E,), jnp.float32, -0.1, 0.1), -0.1, 0.1)
    dinv_off = jnp.clip(jax.random.uniform(streams_of[7], (E,), jnp.float32, -0.08, 0.08), -0.08, 0.08)
    return {"front": front, "delayed": delayed, "dest": dest, "pivots": pivots, "pair_flags": pair_flags, "linv": linv, "dinv_diag": dinv_diag, "dinv_off": dinv_off}


precise = lax.Precision.HIGHEST


def pair_scale(scaled, pair_bits, diag_part, off_part):
    coupled = pair_bits.astype(jnp.float32) * off_part
    zero_col = jnp.zeros_like(scaled[:, :1])
    shifted_next = jnp.concatenate([scaled[:, 1:], zero_col], axis=1)
    shifted_prev = jnp.concatenate([zero_col, scaled[:, :-1]], axis=1)
    coupled_prev = jnp.concatenate([jnp.zeros_like(coupled[:1]), coupled[:-1]])
    return scaled * diag_part + shifted_next * coupled + shifted_prev * coupled_prev


def reference(front, delayed, dest, pivots, pair_flags, linv, dinv_diag, dinv_off):
    targets = pivots[dest]
    current = front.at[:, targets].add(jnp.transpose(delayed))
    factors = []
    for panel_index in range(PANELS):
        offset = panel_index * PANEL
        chosen = pivots[offset:offset + PANEL]
        panel_cols = current[:, chosen]
        scaled = jnp.dot(panel_cols, jnp.transpose(linv[panel_index]), precision=precise)
        columns = pair_scale(scaled, pair_flags[offset:offset + PANEL], dinv_diag[offset:offset + PANEL], dinv_off[offset:offset + PANEL])
        current = current - jnp.dot(columns, jnp.transpose(scaled), precision=precise)
        factors.append(columns)
    retained = jnp.ones((NF,), jnp.float32).at[pivots].set(0.0)
    trailing = current * retained[:, None] * retained[None, :]
    return trailing, jnp.concatenate(factors, axis=1)
```

```python
import functools

import jax
import jax.numpy as jnp
from jax import lax
from jax.experimental import pallas as pl
from jax.experimental.pallas import tpu as pltpu
from jax.sharding import PartitionSpec as P

MESH = pl.DeviceIdType.MESH
VMEM_LIMIT = 60 * 1024 * 1024


def dot(a, b, ca, cb):
    return lax.dot_general(a, b, (((ca,), (cb,)), ((), ())), precision=lax.Precision.HIGHEST)


def pick(ones, a, c1, ca):
    total = None
    for _ in range(3):
        part = lax.reduce_precision(a, 8, 7)
        a = a - part
        term = lax.dot_general(
            ones.astype(jnp.bfloat16), part.astype(jnp.bfloat16), (((c1,), (ca,)), ((), ())),
            preferred_element_type=jnp.float32,
        )
        total = term if total is None else total + term
    return total


def onehot(a, b):
    return (a[:, None] == b[None, :]).astype(jnp.float32)


def pair_scale(scaled, panel_width, pair_flags, diag_part, off_part):
    total = scaled.shape[1]
    slot = lax.broadcasted_iota(jnp.int32, (total,), 0) % panel_width
    coupled = pair_flags.astype(jnp.float32) * off_part
    up = jnp.where(slot == panel_width - 1, 0.0, coupled)
    down = jnp.where(slot == 0, 0.0, jnp.roll(coupled, 1))
    nxt = jnp.roll(scaled, -1, axis=1)
    prv = jnp.roll(scaled, 1, axis=1)
    return scaled * diag_part + nxt * up + prv * down


def gather_kernel(zs, xs, ys, halves, own_ref, all_ref, col_ref, copy_sem, root_sem, all_send, all_recv, col_send, col_recv):
    row, col = lax.axis_index("row"), lax.axis_index("col")
    y, k = row // 2, row % 2
    z, x = col // xs, col % xs
    root = col // halves
    half = col % halves
    root_y, root_k = root // 2, root % 2
    is_root = row == root
    at_root_core = k == root_k

    def at(y_, k_, z_, x_):
        return (y_ * 2 + k_, z_ * xs + x_)

    links = [
        (z + 1 < zs, at(y, k, z + 1, x)),
        (z >= 1, at(y, k, z - 1, x)),
        (x + 1 < xs, at(y, k, z, x + 1)),
        (x >= 1, at(y, k, z, x - 1)),
        (y + 1 < ys, at(y + 1, k, z, x)),
        (y >= 1, at(y - 1, k, z, x)),
        (True, at(y, 1 - k, z, x)),
    ]

    def when(cond, fn):
        if cond is True:
            fn()
        else:
            pl.when(cond)(fn)

    barrier = pltpu.get_barrier_semaphore()
    for cond, dev in links:
        when(cond, lambda dev=dev: pl.semaphore_signal(barrier, inc=1, device_id=dev, device_id_type=MESH))
    peers = 1
    for cond, _ in links[:6]:
        peers = peers + jnp.where(cond, 1, 0)
    pl.semaphore_wait(barrier, peers)

    def block(b, c):
        return all_ref.at[b, c]

    def send_all(way, b, c, src, act):
        act(pltpu.make_async_remote_copy(
            src_ref=src, dst_ref=block(b, c), send_sem=all_send.at[way, b, c], recv_sem=all_recv.at[b, c],
            device_id=links[way][1], device_id_type=MESH))

    def send_col(way, c, src, act):
        act(pltpu.make_async_remote_copy(
            src_ref=src, dst_ref=col_ref.at[c], send_sem=col_send.at[way, c], recv_sem=col_recv.at[c],
            device_id=links[4 + way][1], device_id_type=MESH))

    def arrived(b, c):
        pltpu.make_async_copy(block(b, c), block(b, c), all_recv.at[b, c]).wait()

    def spread_col(c, src, up, down, act):
        when((y + 1 < ys) & up, lambda: send_col(0, c, src, act))
        when((y >= 1) & down, lambda: send_col(1, c, src, act))
        send_col(2, c, src, act)

    def on_block(c, mine, act, draining):
        def go():
            src = own_ref.at[half] if mine else block(half, c)
            spread_col(c, src, True, True, act)
            local = pltpu.make_async_copy(src, col_ref.at[c], root_sem.at[c])
            if draining:
                local.wait()
            else:
                local.start()
        when(is_root, go)

    def on_col(c, act, draining):
        def go():
            if not draining:
                pltpu.make_async_copy(col_ref.at[c], col_ref.at[c], col_recv.at[c]).wait()
            spread_col(c, col_ref.at[c], y > root_y, y < root_y, act)
        when(at_root_core & (y != root_y), go)

    def steps(act, draining):
        pending = []

        def later(cond, c):
            pending.append((cond, c))
            if len(pending) > 3:
                flush()

        def flush():
            cond, c = pending.pop(0)
            when(cond, lambda: on_col(c, act, draining))

        for t in range(zs + xs - 1):
            if t < zs:
                for sign in ((0,) if t == 0 else (-1, 1)):
                    zc = z + sign * t
                    here = True if t == 0 else (zc >= 0) & (zc < zs)
                    c = zc * xs + x

                    def go(c=c, sign=sign, t=t):
                        for b in range(halves):
                            if t and not draining:
                                arrived(b, c)
                            src = own_ref.at[b] if t == 0 else block(b, c)
                            when(x + 1 < xs, lambda: send_all(2, b, c, src, act))
                            when(x >= 1, lambda: send_all(3, b, c, src, act))
                            if sign <= 0:
                                when(z + 1 < zs, lambda: send_all(0, b, c, src, act))
                            if sign >= 0:
                                when(z >= 1, lambda: send_all(1, b, c, src, act))
                        on_block(c, t == 0, act, draining)
                    when(here, go)
                    later(here, c)
            for d in range(1, xs):
                tz = t - d
                if tz < 0 or tz >= zs:
                    continue
                for sign in ((0,) if tz == 0 else (-1, 1)):
                    for side in (-1, 1):
                        zc, xc = z + sign * tz, x + side * d
                        here = (zc >= 0) & (zc < zs) & (xc >= 0) & (xc < xs)
                        c = zc * xs + xc

                        def go(c=c, side=side):
                            for b in range(halves):
                                if not draining:
                                    arrived(b, c)
                                if side < 0:
                                    when(x + 1 < xs, lambda: send_all(2, b, c, block(b, c), act))
                                else:
                                    when(x >= 1, lambda: send_all(3, b, c, block(b, c), act))
                            on_block(c, False, act, draining)
                        when(here, go)
                        later(here, c)
        while pending:
            flush()

    keep = [pltpu.make_async_copy(own_ref.at[b], block(b, col), copy_sem.at[b]) for b in range(halves)]
    for copy in keep:
        copy.start()
    steps(lambda copy: copy.start(), False)
    for copy in keep:
        copy.wait()
    steps(lambda copy: copy.wait_send(), True)

    def last():
        for c in range(zs * xs):
            pltpu.make_async_copy(col_ref.at[c], col_ref.at[c], col_recv.at[c]).wait()
    when(k != root_k, last)


def exchange(own, halves, height):
    n_col = lax.axis_size("col")
    n_row = lax.axis_size("row")
    slots = own.shape[1]
    ys = n_row // 2
    xs = ys if n_col % ys == 0 else 1
    zs = n_col // xs
    vmem = pl.BlockSpec(memory_space=pltpu.VMEM)
    every, cols = pl.pallas_call(
        functools.partial(gather_kernel, zs, xs, ys, halves),
        out_shape=(
            jax.ShapeDtypeStruct((halves, n_col, height, slots), jnp.float32),
            jax.ShapeDtypeStruct((n_col, height, slots), jnp.float32),
        ),
        in_specs=[vmem],
        out_specs=(vmem, vmem),
        scratch_shapes=[
            pltpu.SemaphoreType.DMA((halves,)),
            pltpu.SemaphoreType.DMA((n_col,)),
            pltpu.SemaphoreType.DMA((4, halves, n_col)),
            pltpu.SemaphoreType.DMA((halves, n_col)),
            pltpu.SemaphoreType.DMA((3, n_col)),
            pltpu.SemaphoreType.DMA((n_col,)),
        ],
        compiler_params=pltpu.CompilerParams(
            collective_id=0, has_side_effects=True, vmem_limit_bytes=VMEM_LIMIT
        ),
    )(own.reshape(halves, height, slots))
    return every.reshape(halves * n_col * height, slots), cols.reshape(n_col * height, slots)


def trailing_kernel(tile, s_ref, c_ref, front_ref, rkeep_ref, ckeep_ref, coef_ref, out_ref, factor_ref, chi, clo):
    slots = s_ref.shape[1]
    cols = c_ref.shape[0]

    @pl.when(pl.program_id(0) == 0)
    def _():
        @pl.loop(0, cols // tile)
        def _(i):
            part = pl.ds(pl.multiple_of(i * tile, tile), tile)
            block = c_ref[part, :].T
            hi = block.astype(jnp.bfloat16)
            chi[:, part] = hi
            clo[:, part] = (block - hi.astype(jnp.float32)).astype(jnp.bfloat16)

    s = s_ref[...]
    columns = (
        s * coef_ref[0:1, :]
        + pltpu.roll(s, slots - 1, 1) * coef_ref[1:2, :]
        + pltpu.roll(s, 1, 1) * coef_ref[2:3, :]
    )
    factor_ref[...] = columns
    hi = columns.astype(jnp.bfloat16)
    lo = (columns - hi.astype(jnp.float32)).astype(jnp.bfloat16)
    rkeep = rkeep_ref[...] > 0.0

    @pl.loop(0, cols // tile)
    def _(i):
        part = pl.ds(pl.multiple_of(i * tile, tile), tile)
        bh, bl = chi[:, part], clo[:, part]
        acc = jnp.dot(hi, bh, preferred_element_type=jnp.float32)
        acc += jnp.dot(hi, bl, preferred_element_type=jnp.float32)
        acc += jnp.dot(lo, bh, preferred_element_type=jnp.float32)
        out_ref[:, part] = jnp.where(rkeep & (ckeep_ref[:, part] > 0.0), front_ref[:, part] - acc, 0.0)


def update(every, col_scaled, front, row_keep, col_keep, coef):
    rows, cols = front.shape
    slots = every.shape[1]
    tile = 256
    return pl.pallas_call(
        functools.partial(trailing_kernel, tile),
        grid=(rows // tile,),
        in_specs=[
            pl.BlockSpec((tile, slots), lambda i: (i, 0)),
            pl.BlockSpec((cols, slots), lambda i: (0, 0)),
            pl.BlockSpec((tile, cols), lambda i: (i, 0)),
            pl.BlockSpec((tile, 1), lambda i: (i, 0)),
            pl.BlockSpec((1, cols), lambda i: (0, 0)),
            pl.BlockSpec((8, slots), lambda i: (0, 0)),
        ],
        out_specs=(
            pl.BlockSpec((tile, cols), lambda i: (i, 0)),
            pl.BlockSpec((tile, slots), lambda i: (i, 0)),
        ),
        out_shape=(
            jax.ShapeDtypeStruct((rows, cols), jnp.float32),
            jax.ShapeDtypeStruct((rows, slots), jnp.float32),
        ),
        scratch_shapes=[pltpu.VMEM((slots, cols), jnp.bfloat16), pltpu.VMEM((slots, cols), jnp.bfloat16)],
        compiler_params=pltpu.CompilerParams(
            dimension_semantics=("arbitrary",), vmem_limit_bytes=VMEM_LIMIT
        ),
    )(every, col_scaled, front, row_keep, col_keep, coef)


def body(front, delayed, dest, pivots, pair_flags, linv, dinv_diag, dinv_off):
    n_col = lax.axis_size("col")
    n_row = lax.axis_size("row")
    rows_blk, cols_blk = front.shape
    row_id = lax.axis_index("row")
    col_id = lax.axis_index("col")
    row_start = row_id * rows_blk
    col_start = col_id * cols_blk
    panels, width, _ = linv.shape
    slots = pivots.shape[0]
    per_col = slots // n_col
    per_row = slots // n_row
    ndel = delayed.shape[0]
    halves = rows_blk // cols_blk
    height = cols_blk // n_col
    slot_ids = jnp.arange(slots, dtype=jnp.int32)

    col_owner = pivots // cols_blk
    row_owner = pivots // rows_blk
    before = slot_ids[None, :] < slot_ids[:, None]
    col_rank = jnp.sum((before & (col_owner[:, None] == col_owner[None, :])).astype(jnp.int32), axis=1)
    row_rank = jnp.sum((before & (row_owner[:, None] == row_owner[None, :])).astype(jnp.int32), axis=1)
    col_rel = jnp.where(col_owner == col_id, pivots - col_start, -1)
    row_rel = jnp.where(row_owner == row_id, pivots - row_start, -1)
    col_want = jnp.sum(
        jnp.where((col_owner == col_id)[None, :] & (col_rank[None, :] == jnp.arange(per_col)[:, None]), col_rel[None, :], 0),
        axis=1,
    )
    row_want = jnp.sum(
        jnp.where((row_owner == row_id)[None, :] & (row_rank[None, :] == jnp.arange(per_row)[:, None]), row_rel[None, :], 0),
        axis=1,
    )

    picked = pick(onehot(col_want, jnp.arange(cols_blk)), front, 1, 1)
    mine = jnp.concatenate([picked, delayed], axis=0)
    wide = per_col + ndel

    piv_part = pick(onehot(row_want, jnp.arange(rows_blk)), mine, 1, 1).T
    slot_row = jnp.pad(dest.astype(jnp.float32)[None, :], ((0, 7), (0, per_row - ndel)))
    piv_all = lax.all_gather(jnp.concatenate([piv_part, slot_row], axis=0), ("row", "col"), axis=0, tiled=False)
    piv_all = piv_all.reshape(n_row, n_col, wide + 8, per_row)
    dest_all = piv_all[0, :, wide, :ndel].astype(jnp.int32)
    piv_all = piv_all[:, :, :wide].reshape(n_row, n_col * wide, per_row)
    share = mine.reshape(wide, halves, n_col, height).transpose(2, 0, 1, 3)
    share = share.reshape(n_col, wide, halves * height)
    share = lax.all_to_all(share, "col", split_axis=0, concat_axis=0, tiled=True)
    share = share.reshape(n_col * wide, halves * height)

    home = jnp.where(
        jnp.arange(wide)[None, :] < per_col,
        jnp.arange(n_col)[:, None] * per_col + jnp.arange(wide)[None, :],
        -1,
    )
    is_col = home.reshape(-1)[:, None] == (col_owner * per_col + col_rank)[None, :]
    dest_wide = jnp.concatenate([jnp.full((n_col, per_col), -1, jnp.int32), dest_all], axis=1)
    is_del = dest_wide.reshape(-1)[:, None] == slot_ids[None, :]
    take = (is_col | is_del).astype(jnp.float32)
    stacked = jnp.concatenate([piv_all[r] for r in range(n_row)] + [share], axis=1)
    current = dot(stacked, take, 0, 0)
    to_slot = onehot(row_owner * per_row + row_rank, slot_ids)

    done = []
    parts = []
    for p in range(panels):
        lo, hi = p * width, (p + 1) * width
        cols = current[:, lo:hi]
        for earlier_cols, earlier_rows, start in done:
            cols = cols - dot(earlier_cols, earlier_rows[lo - start : hi - start], 1, 1)
        scaled = dot(cols, linv[p], 1, 1)
        parts.append(scaled[slots:])
        if p + 1 < panels:
            columns = pair_scale(scaled, width, pair_flags[lo:hi], dinv_diag[lo:hi], dinv_off[lo:hi])
            rows = pick(to_slot[hi:], scaled[:slots], 1, 0)
            done.append((columns, rows, hi))
    own = jnp.concatenate(parts, axis=1)

    every, col_scaled = exchange(own, halves, height)
    in_panel = slot_ids % width
    coupled = pair_flags.astype(jnp.float32) * dinv_off
    zero = jnp.zeros_like(dinv_diag)
    coef = jnp.stack(
        [dinv_diag, jnp.where(in_panel == width - 1, 0.0, coupled), jnp.where(in_panel == 0, 0.0, jnp.roll(coupled, 1))]
        + [zero] * 5
    )
    row_in = jnp.any((row_start + jnp.arange(rows_blk))[:, None] == pivots[None, :], axis=1)
    col_in = jnp.any((col_start + jnp.arange(cols_blk))[:, None] == pivots[None, :], axis=1)
    row_keep = jnp.where(row_in, 0.0, 1.0)[:, None]
    col_keep = jnp.where(col_in, 0.0, 1.0)[None, :]
    trailing, factor = update(every, col_scaled, front, row_keep, col_keep, coef)
    return (trailing, factor)


def solution(mesh):
    return jax.shard_map(
        body,
        mesh=mesh,
        in_specs=(P("row", "col"), P("col", "row"), P("col"), P(), P(), P(), P(), P()),
        out_specs=(P("row", "col"), P("row", None)),
        check_vma=False,
    )
```
